32 devices in a mesh: row: 4 (over y, x), col: 8 (over z, core).
Axes of the slice: x: 2, y: 2, z: 4, core: 2. Of those that a mesh axis runs over, the one named last changes fastest.
Arguments:
- inv_sep: bfloat16 [24576, 24576], P('row', 'col'), may hold values from -6 to 6
- lower_one: bfloat16 [24576, 256], P('col', 'row'), may hold values from -0.078125 to 0.078125
- upper_one: bfloat16 [256, 24576], P('col', 'row'), may hold values from -0.078125 to 0.078125
- diag_inv_one: float32 [256, 256], replicated, may hold values from -6 to 6
- blocks_one: int32 [40], replicated, may hold values from 0 to 191, as said below
- lower_two: bfloat16 [24576, 256], P('col', 'row'), may hold values from -0.09375 to 0.09375
- upper_two: bfloat16 [256, 24576], P('col', 'row'), may hold values from -0.09375 to 0.09375
- corner_lower: bfloat16 [256, 256], replicated, may hold values from -0.375 to 0.375
- corner_upper: bfloat16 [256, 256], replicated, may hold values from -0.375 to 0.375
- diag_inv_two: float32 [256, 256], replicated, may hold values from -6 to 6
- blocks_two: int32 [32], replicated, may hold values from 0 to 191, as said below
Outputs:
- inv_lower_one: bfloat16 [5120, 256], P(('row', 'col'))
- inv_upper_one: bfloat16 [256, 5120], P('row', 'col')
- inv_diag_one: float32 [256, 256], replicated
- inv_lower_two: bfloat16 [4096, 256], P(('row', 'col'))
- inv_upper_two: bfloat16 [256, 4096], P('row', 'col')
- inv_diag_two: float32 [256, 256], replicated
The draws below stay inside these ranges and needn't reach their ends.
Inputs may be any that keep to these rules, and one draw needn't show every extreme that they name: `blocks_one`: distinct block indices in increasing order; each aligned run of 24 blocks holds exactly 5 of them; the first and the last block of the separator are listed. `blocks_two`: distinct block indices in increasing order, each of them also in blocks_one; each aligned run of 24 blocks holds exactly 4 of them; the first and the last block of the separator are listed.
All inputs are finite; a program needn't handle non-finite values.
Results may differ from the reference program's by a relative error of at most 0.0039.
Values may be sent and summed in bfloat16 or wider, within the bound.
No kernel may reach another device: no remote copies, remote signals or barrier semaphores. Data moves between devices by JAX's collectives and lax.ppermute only.
A program may use at most 128 MiB of HBM per device.

```python
import jax
import jax.numpy as jnp
from jax import lax

NS = 24576
W = 256
B = 128
SPAN = 24
PICK_ONE = 5
PICK_TWO = 4
LIST_ONE = 40
LIST_TWO = 32


def block_lists(key):
    run_count = NS // B // SPAN
    run_keys = jax.random.split(key, 2 * run_count)

    def one_run(run_id, head_key, tail_key):
        random_head = jax.random.randint(head_key, (), 0, SPAN)
        head_block = jnp.where(run_id == 0, 0, jnp.where(run_id == run_count - 1, SPAN - 1, random_head)).astype(jnp.int32)
        tail_blocks = jax.random.permutation(tail_key, SPAN - 1).astype(jnp.int32)
        tail_blocks = tail_blocks + (tail_blocks >= head_block).astype(jnp.int32)
        ordering = jnp.concatenate([head_block[None], tail_blocks])
        listed_one = run_id * SPAN + jnp.sort(ordering[:PICK_ONE])
        listed_two = run_id * SPAN + jnp.sort(ordering[:PICK_TWO])
        return (listed_one, listed_two)
    listed_one, listed_two = jax.vmap(one_run)(jnp.arange(run_count, dtype=jnp.int32), run_keys[:run_count], run_keys[run_count:])
    return (listed_one.reshape(-1).astype(jnp.int32), listed_two.reshape(-1).astype(jnp.int32))


def draw_blocks_one(key, part):
    return block_lists(jax.random.fold_in(key, 11))[0]


def draw_blocks_two(key, part):
    return block_lists(jax.random.fold_in(key, 11))[1]


def with_spikes(array, rng, source, target, shards_of, factor):
    owner, partner = [(jnp.arange(array.shape[dim]) // (array.shape[dim] // shards_of)).reshape([-1 if axis == dim else 1 for axis in range(array.ndim)]) for dim in (source, target)]
    chosen = jax.random.permutation(rng, shards_of)[partner]
    strong = (owner == chosen) | (owner == (partner + shards_of // 2) % shards_of)
    return jnp.where(strong, factor * array, array)


def levels(key, dims, cuts, smallest, high):
    factor_of, own = 1.0, jax.random.fold_in(key, 6)
    for position, shards_of in cuts:
        heights = jnp.exp(jax.random.uniform(jax.random.fold_in(own, position), (shards_of,), jnp.float32, smallest / len(cuts), high / len(cuts)))
        factor_of = factor_of * jnp.repeat(heights, dims[position] // shards_of).reshape([-1 if axis == position else 1 for axis in range(len(dims))])
    return factor_of


def scatter_about(own_key, shape, width, reach, cuts=(), kind=jnp.bfloat16):
    drawn = width * jax.random.normal(own_key, shape, jnp.float32)
    if cuts:
        drawn = drawn * levels(own_key, shape, cuts, -0.22, 0.18)
    return jnp.clip(drawn, -reach, reach).astype(kind)


def heavy_noise(stream_key, extent, deviation, reach, cuts, heavy, held_as=jnp.bfloat16):
    array = deviation * jax.random.normal(stream_key, extent, jnp.float32)
    if cuts:
        array = array * levels(stream_key, extent, cuts, -0.22, 0.18)
    return jnp.clip(with_spikes(array, jax.random.fold_in(stream_key, 3), *heavy), -reach, reach).astype(held_as)


def setup_inputs(seed: int = 0) -> dict:
    seeds = jax.random.split(jax.random.key(seed), 12)
    inv_sep = heavy_noise(seeds[0], (NS, NS), 1.0, 6.0, ((0, 4), (1, 8)), (1, 0, 8, 2.0))
    lower_one = scatter_about(seeds[1], (NS, W), (LIST_ONE * B) ** -0.5, 0.078125, ((0, 8), (1, 4)))
    upper_one = scatter_about(seeds[2], (W, NS), (LIST_ONE * B) ** -0.5, 0.078125, ((0, 8), (1, 4)))
    diag_inv_one = scatter_about(seeds[3], (W, W), 1.0, 6.0, (), jnp.float32)
    blocks_one = draw_blocks_one(jax.random.fold_in(seeds[11], 71), 0)
    lower_two = scatter_about(seeds[5], (NS, W), (LIST_TWO * B) ** -0.5, 0.09375, ((0, 8), (1, 4)))
    upper_two = scatter_about(seeds[6], (W, NS), (LIST_TWO * B) ** -0.5, 0.09375, ((0, 8), (1, 4)))
    corner_lower = scatter_about(seeds[7], (W, W), W ** -0.5, 0.375)
    corner_upper = scatter_about(seeds[8], (W, W), W ** -0.5, 0.375)
    diag_inv_two = scatter_about(seeds[9], (W, W), 1.0, 6.0, (), jnp.float32)
    blocks_two = draw_blocks_two(jax.random.fold_in(seeds[11], 71), 0)
    return {"inv_sep": inv_sep, "lower_one": lower_one, "upper_one": upper_one, "diag_inv_one": diag_inv_one, "blocks_one": blocks_one, "lower_two": lower_two, "upper_two": upper_two, "corner_lower": corner_lower, "corner_upper": corner_upper, "diag_inv_two": diag_inv_two, "blocks_two": blocks_two}


def block_rows(blocks):
    return (blocks[:, None] * B + jnp.arange(B, dtype=jnp.int32)[None, :]).reshape(-1).astype(jnp.int32)


def highest(first_mat, second_mat):
    return jnp.dot(first_mat.astype(jnp.float32), second_mat.astype(jnp.float32), precision=lax.Precision.HIGHEST)


def rows_times(inv_sep, blocks, panel_mat):
    columns = block_rows(blocks)

    def one_block(block_id):
        row_block = lax.dynamic_slice_in_dim(inv_sep, (block_id * B).astype(jnp.int32), B, 0)
        return highest(jnp.take(row_block, columns, axis=1), panel_mat)

    return lax.map(one_block, blocks).reshape(blocks.shape[0] * B, panel_mat.shape[1])


def left_times(panel_mat, inv_sep, blocks):
    columns = block_rows(blocks)
    pieces = jnp.transpose(panel_mat.reshape(panel_mat.shape[0], blocks.shape[0], B), (1, 0, 2))

    def add_block(summed, paired):
        row_block = lax.dynamic_slice_in_dim(inv_sep, (paired[0] * B).astype(jnp.int32), B, 0)
        return summed + highest(paired[1], jnp.take(row_block, columns, axis=1)), None

    summed, _ = lax.scan(add_block, jnp.zeros((panel_mat.shape[0], columns.shape[0]), jnp.float32), (blocks, pieces))
    return summed


def reference(inv_sep, lower_one, upper_one, diag_inv_one, blocks_one, lower_two, upper_two, corner_lower, corner_upper, diag_inv_two, blocks_two):
    rows_one = block_rows(blocks_one)
    rows_two = block_rows(blocks_two)
    places = jnp.sum((blocks_one[None, :] < blocks_two[:, None]).astype(jnp.int32), axis=1).astype(jnp.int32)
    positions = block_rows(places)
    lower_p = jnp.take(lower_one, rows_one, axis=0)
    upper_p = jnp.take(upper_one, rows_one, axis=1)
    lower_c = jnp.take(lower_two, rows_two, axis=0)
    upper_c = jnp.take(upper_two, rows_two, axis=1)
    inv_lower_one = (-rows_times(inv_sep, blocks_one, lower_p)).astype(jnp.bfloat16)
    inv_upper_one = (-left_times(upper_p, inv_sep, blocks_one)).astype(jnp.bfloat16)
    inv_diag_one = diag_inv_one - highest(upper_p, inv_lower_one)
    ancestor_rows = jnp.take(inv_lower_one, positions, axis=0)
    ancestor_cols = jnp.take(inv_upper_one, positions, axis=1)
    inv_lower_two = (-(rows_times(inv_sep, blocks_two, lower_c) + highest(ancestor_rows, corner_lower))).astype(jnp.bfloat16)
    inv_upper_two = (-(left_times(upper_c, inv_sep, blocks_two) + highest(corner_upper, ancestor_cols))).astype(jnp.bfloat16)
    corner_inv = -(highest(ancestor_cols, lower_c) + highest(inv_diag_one, corner_lower))
    inv_diag_two = diag_inv_two - (highest(upper_c, inv_lower_two) + highest(corner_upper, corner_inv))
    return inv_lower_one, inv_upper_one, inv_diag_one, inv_lower_two, inv_upper_two, inv_diag_two
```

```python
import jax
import jax.numpy as jnp
from jax import lax
from jax.experimental import pallas as pl
from jax.experimental.pallas import tpu as pltpu
from jax.sharding import PartitionSpec as P

B = 128
F32 = jnp.float32
BF16 = jnp.bfloat16

PAIR_TYPE = F32
Z_TYPE = BF16
ROW_TYPE = BF16
DIAG_PAIR = F32
DIAG_Z = BF16
DIAG_OUT = BF16

NT = (((1,), (1,)), ((), ()))
TN = (((0,), (0,)), ((), ()))


def dot(a, b):
    return jnp.dot(a, b, preferred_element_type=F32)


def split(x):
    high = x.astype(BF16)
    return high, (x - high.astype(F32)).astype(BF16)


def exchange(x, axis, size, distance):
    return lax.ppermute(x, axis, [(s, s ^ distance) for s in range(size)])


def in_hbm(x):
    return pltpu.with_memory_space_constraint(x, pltpu.HBM)


def shape(dims, dtype):
    return jax.ShapeDtypeStruct(dims, dtype)


VMEM = pl.BlockSpec(memory_space=pltpu.VMEM)
SMEM = pl.BlockSpec(memory_space=pltpu.SMEM)
HBM = pl.BlockSpec(memory_space=pltpu.HBM)


def call(body, in_specs, outs, scratch=(), mib=8):
    return pl.pallas_call(
        body,
        out_shape=tuple(outs),
        in_specs=in_specs,
        out_specs=tuple(VMEM for _ in outs),
        scratch_shapes=list(scratch),
        compiler_params=pltpu.CompilerParams(vmem_limit_bytes=mib << 20),
    )


def on_device(
    inv_sep,
    lower_one,
    upper_one,
    diag_inv_one,
    blocks_one,
    lower_two,
    upper_two,
    corner_lower,
    corner_upper,
    diag_inv_two,
    blocks_two,
):
    nr, nc = lax.axis_size("row"), lax.axis_size("col")
    nz = nc // 2
    blocks_one, blocks_two = in_hbm(blocks_one), in_hbm(blocks_two)
    rows_here, cols_here = inv_sep.shape
    width = diag_inv_one.shape[0]
    run_blocks = cols_here // B
    p1, p2 = blocks_one.shape[0] // nc, blocks_two.shape[0] // nc
    runs = nc // nr
    g1, g2 = p1 * runs, p2 * runs
    n1, n2 = p1 * B, p2 * B
    m1, m2 = g1 * B, g2 * B
    s1, s2 = m1 // nc, m2 // nc
    lw, uw, rw = width // nr, width // nc, width // nr
    unit = min(B, s2)

    def place_col(one, two, b):
        j = lax.axis_index("col")
        block = two[j * p2 + b]
        return sum((one[j * p1 + a] < block).astype(jnp.int32) for a in range(p1))

    def place_row(one, two, k):
        i = lax.axis_index("row")
        run = k // p2
        block = two[i * g2 + k]
        return run * p1 + sum((one[i * g1 + run * p1 + a] < block).astype(jnp.int32) for a in range(p1))

    def pick_panels(one, two, low1, low2, up1, up2, low, up, sems):
        i, j = lax.axis_index("row"), lax.axis_index("col")

        def lanes(block):
            return pl.ds(pl.multiple_of(block * B, B), B)

        for a in range(p1):
            pltpu.make_async_copy(
                low1.at[:, lanes(one[j * p1 + a] - j * run_blocks)], low.at[:, pl.ds(a * B, B)], sems.at[0]
            ).start()
        for a in range(p2):
            pltpu.make_async_copy(
                low2.at[:, lanes(two[j * p2 + a] - j * run_blocks)], low.at[:, pl.ds(n1 + a * B, B)], sems.at[0]
            ).start()
        for a in range(g1):
            pltpu.make_async_copy(
                up1.at[:, lanes(one[i * g1 + a] - i * (rows_here // B))], up.at[:, pl.ds(a * B, B)], sems.at[1]
            ).start()
        for a in range(g2):
            pltpu.make_async_copy(
                up2.at[:, lanes(two[i * g2 + a] - i * (rows_here // B))], up.at[:, pl.ds(m1 + a * B, B)], sems.at[1]
            ).start()
        pltpu.make_async_copy(low, low, sems.at[0]).wait()
        pltpu.make_async_copy(up, up, sems.at[1]).wait()

    low, up = call(
        pick_panels,
        [SMEM, SMEM, HBM, HBM, HBM, HBM],
        [shape((lw, n1 + n2), BF16), shape((uw, m1 + m2), BF16)],
        [pltpu.SemaphoreType.DMA((2,))],
    )(blocks_one, blocks_two, *map(in_hbm, (lower_one.T, lower_two.T, upper_one, upper_two)))

    ups = [up] + [exchange(up, "col", nc, 2 * k) for k in range(1, nz)]
    lows = [low] + [exchange(low, "row", nr, k) for k in range(1, nr)]
    others = [exchange(u, "col", nc, 1) for u in ups]

    def pick_sep(one, whole, d1, d2, cl, cu, sep, base, sem):
        i, j = lax.axis_index("row"), lax.axis_index("col")
        for a in range(g1):
            r = pl.multiple_of((one[i * g1 + a] - i * (rows_here // B)) * B, B)
            for b in range(p1):
                c = pl.multiple_of((one[j * p1 + b] - j * run_blocks) * B, B)
                pltpu.make_async_copy(
                    whole.at[pl.ds(r, B), pl.ds(c, B)], sep.at[pl.ds(a * B, B), pl.ds(b * B, B)], sem
                ).start()
        inner = jnp.dot(d1[...], cl[...].astype(F32), precision=lax.Precision.HIGHEST, preferred_element_type=F32)
        base[...] = d2[...] + jnp.dot(
            cu[...].astype(F32), inner, precision=lax.Precision.HIGHEST, preferred_element_type=F32
        )
        pltpu.make_async_copy(sep, sep, sem).wait()

    sep, base = call(
        pick_sep,
        [SMEM, HBM, VMEM, VMEM, VMEM, VMEM],
        [shape((m1, n1), BF16), shape((width, width), F32)],
        [pltpu.SemaphoreType.DMA],
    )(blocks_one, in_hbm(inv_sep), diag_inv_one, diag_inv_two, corner_lower, corner_upper)

    def lower_products(*refs):
        one, two = refs[:2]
        parts = refs[2 : 2 + nr]
        sep, cl, first_out, high_out, low_out, own, send, panel, ext, prod1, prod2 = refs[2 + nr :]
        i, j = lax.axis_index("row"), lax.axis_index("col")
        for k in range(nr):
            panel[pl.ds(pl.multiple_of((i ^ k) * lw, lw), lw), :] = parts[k][...].astype(F32)
        first = panel[:, :n1].astype(BF16)
        ext[...] = jnp.zeros_like(ext)
        for b in range(p2):
            spot = pl.multiple_of(place_col(one, two, b) * B, B)
            ext[:, pl.ds(spot, B)] = panel[:, n1 + b * B : n1 + (b + 1) * B]
        second = ext[...] - lax.dot_general(cl[...], first, TN, preferred_element_type=F32)
        high, low = split(second)
        first_out[...] = first
        high_out[...] = high
        low_out[...] = low
        s = sep[...]
        prod1[...] = lax.dot_general(s, first, NT, preferred_element_type=F32)
        prod2[...] = lax.dot_general(s, high, NT, preferred_element_type=F32) + lax.dot_general(
            s, low, NT, preferred_element_type=F32
        )
        for core in range(2):
            target = own if core == 0 else send
            for k in range(nz):
                owner = j ^ (2 * k + core)
                target[k, :s1, :] = prod1[pl.ds(pl.multiple_of(owner * s1, 16), s1), :].astype(target.dtype)
                for v in range(s2 // unit):
                    row = owner * s2 + v * unit
                    spot = place_row(one, two, row // B) * B + row % B
                    target[k, s1 + v * unit : s1 + (v + 1) * unit, :] = prod2[
                        pl.ds(pl.multiple_of(spot, unit), unit), :
                    ].astype(target.dtype)

    first_l, high_l, low_l, own, send = call(
        lower_products,
        [SMEM, SMEM] + [VMEM] * (nr + 2),
        [shape((width, n1), BF16)] * 3
        + [
            shape((nz, s1 + s2, width), F32),
            shape((nz, s1 + s2, width), PAIR_TYPE),
        ],
        [
            pltpu.VMEM((width, n1 + n2), F32),
            pltpu.VMEM((width, n1), F32),
            pltpu.VMEM((m1, width), F32),
            pltpu.VMEM((m1, width), F32),
        ],
        mib=32,
    )(blocks_one, blocks_two, *lows, sep, corner_lower)

    got = exchange(send, "col", nc, 1)

    def upper_products(*refs):
        one, two = refs[:2]
        parts = refs[2 : 2 + nc]
        cu, sep, mine = refs[2 + nc : 5 + nc]
        sends = refs[5 + nc : 4 + nc + nr]
        panel, ext, total = refs[4 + nc + nr :]
        i, j = lax.axis_index("row"), lax.axis_index("col")
        for k in range(nc):
            owner = j ^ (2 * (k % nz) + k // nz)
            panel[pl.ds(pl.multiple_of(owner * uw, uw), uw), :] = parts[k][...].astype(F32)
        ext[...] = jnp.zeros_like(ext)
        for b in range(g2):
            spot = pl.multiple_of(place_row(one, two, b) * B, B)
            ext[:, pl.ds(spot, B)] = panel[:, m1 + b * B : m1 + (b + 1) * B]
        first = panel[:, :m1].astype(BF16)
        high, low = split(ext[...] - dot(cu[...], first))
        s = sep[...]
        total[:, :n1] = dot(first, s)
        total[:, n1:] = dot(high, s) + dot(low, s)
        for k in range(nr):
            rows = pl.ds(pl.multiple_of((i ^ k) * rw, rw), rw)
            out = mine if k == 0 else sends[k - 1]
            out[...] = total[rows, :].astype(out.dtype)

    umine, *usends = call(
        upper_products,
        [SMEM, SMEM] + [VMEM] * (nc + 2),
        [shape((rw, 2 * n1), F32)] + [shape((rw, 2 * n1), ROW_TYPE)] * (nr - 1),
        [
            pltpu.VMEM((width, m1 + m2), F32),
            pltpu.VMEM((width, m1), F32),
            pltpu.VMEM((width, 2 * n1), F32),
        ],
        mib=32,
    )(blocks_one, blocks_two, *ups, *others, corner_upper, sep)
    upper_got = [exchange(x, "row", nr, k) for k, x in enumerate(usends, 1)]

    def lower_pair(own, got, mine, *sends):
        mine[...] = own[0] + got[0].astype(F32)
        for k in range(1, nz):
            sends[k - 1][...] = (own[k] + got[k].astype(F32)).astype(Z_TYPE)

    mine, *sends = call(
        lower_pair, [VMEM] * 2, [shape((s1 + s2, width), F32)] + [shape((s1 + s2, width), Z_TYPE)] * (nz - 1), mib=16
    )(own, got)
    lower_got = [exchange(x, "col", nc, 2 * k) for k, x in enumerate(sends, 1)]

    def upper_final(*refs):
        one, two, mine = refs[:3]
        got = refs[3 : 2 + nr]
        lp, lh, ll, out1, out2, keep, send, second, part = refs[2 + nr :]
        total = mine[...]
        for g in got:
            total = total + g[...].astype(F32)
        out1[...] = (-total[:, :n1]).astype(BF16)
        second[...] = -total[:, n1:]
        for b in range(p2):
            spot = pl.multiple_of(place_col(one, two, b) * B, B)
            out2[:, b * B : (b + 1) * B] = second[:, pl.ds(spot, B)].astype(BF16)

        def nt(a, b):
            return lax.dot_general(a, b, NT, preferred_element_type=F32)

        qh, ql = split(total[:, :n1])
        part[0] = nt(qh, lp[...]) + nt(ql, lp[...])
        qh, ql = split(total[:, n1:])
        part[1] = nt(qh, lh[...]) + nt(ql, lh[...]) + nt(qh, ll[...])
        core = lax.axis_index("col") % 2
        keep[...] = part[core]
        send[...] = part[1 - core].astype(DIAG_PAIR)

    inv_upper_one, inv_upper_two, dkeep, dsend = call(
        upper_final,
        [SMEM] * 2 + [VMEM] * (nr + 3),
        [
            shape((rw, n1), BF16),
            shape((rw, n2), BF16),
            shape((rw, width), F32),
            shape((rw, width), DIAG_PAIR),
        ],
        [pltpu.VMEM((rw, n1), F32), pltpu.VMEM((2, rw, width), F32)],
    )(blocks_one, blocks_two, umine, *upper_got, first_l, high_l, low_l)
    dgot = exchange(dsend, "col", nc, 1)

    def diag_pair(keep, got, out):
        out[...] = (keep[...] + got[...].astype(F32)).astype(out.dtype)

    (dpart,) = call(diag_pair, [VMEM] * 2, [shape((rw, width), DIAG_Z)])(dkeep, dgot)
    dz = [dpart] + [exchange(dpart, "col", nc, 2 * k) for k in range(1, nz)]

    def diag_z(*refs):
        parts, out, slots = refs[:nz], refs[nz], refs[nz + 1]
        chip = lax.axis_index("col") // 2
        for k in range(nz):
            slots[chip ^ k] = parts[k][...].astype(F32)
        total = slots[0]
        for k in range(1, nz):
            total = total + slots[k]
        out[...] = total.astype(out.dtype)

    (dsum,) = call(diag_z, [VMEM] * nz, [shape((rw, width), DIAG_OUT)], [pltpu.VMEM((nz, rw, width), F32)])(*dz)
    dall = [dsum] + [exchange(dsum, "row", nr, k) for k in range(1, nr)]
    dother = [exchange(x, "col", nc, 1) for x in dall]

    def lower_final(mine, *refs):
        got, (out1, out2) = refs[:-2], refs[-2:]
        total = mine[...]
        for g in got:
            total = total + g[...].astype(F32)
        out1[...] = (-total[:s1]).astype(BF16)
        out2[...] = (-total[s1:]).astype(BF16)

    inv_lower_one, inv_lower_two = call(
        lower_final, [VMEM] * nz, [shape((s1, width), BF16), shape((s2, width), BF16)]
    )(mine, *lower_got)

    def diag_final(*refs):
        parts, (d1, base, out1, out2) = refs[: 2 * nr], refs[2 * nr :]
        i, core = lax.axis_index("row"), lax.axis_index("col") % 2
        for side in range(2):
            for k in range(nr):
                rows = pl.ds(pl.multiple_of((i ^ k) * rw, rw), rw)
                piece = parts[side * nr + k][...].astype(F32)

                @pl.when((core ^ side) == 0)
                def _():
                    out1[rows, :] = d1[rows, :] + piece

                @pl.when((core ^ side) == 1)
                def _():
                    out2[rows, :] = base[rows, :] + piece

    inv_diag_one, inv_diag_two = call(
        diag_final, [VMEM] * (2 * nr + 2), [shape((width, width), F32)] * 2
    )(*dall, *dother, diag_inv_one, base)
    return (inv_lower_one, inv_upper_one, inv_diag_one, inv_lower_two, inv_upper_two, inv_diag_two)


def solution(mesh):
    return jax.shard_map(
        on_device,
        mesh=mesh,
        in_specs=(
            P("row", "col"),
            P("col", "row"),
            P("col", "row"),
            P(),
            P(),
            P("col", "row"),
            P("col", "row"),
            P(),
            P(),
            P(),
            P(),
        ),
        out_specs=(
            P(("row", "col"), None),
            P("row", "col"),
            P(),
            P(("row", "col"), None),
            P("row", "col"),
            P(),
        ),
        check_vma=False,
    )
```
